768 devices in a mesh: section: 16 (over x, y_hi), seq: 24 (over z, y_lo), dp: 2 (over core).
Axes of the slice: x: 4, y: 8 (y_hi: 4, y_lo: 2; y = y_hi * 2 + y_lo), z: 12, core: 2. Of those that a mesh axis runs over, the one named last changes fastest.
Arguments:
- queries: bfloat16 [32, 3072, 1280], P(('section', 'dp'), 'seq'), may hold values from -5 to 5, as said below
- key_input: bfloat16 [32, 3072, 1280], P(('section', 'dp'), 'seq'), may hold values from -5 to 5
- value_input: bfloat16 [32, 3072, 1280], P(('section', 'dp'), 'seq'), may hold values from -6 to 6
- residual: bfloat16 [32, 3072, 1280], P(('section', 'dp'), 'seq'), may hold values from -4 to 4
- segments: int32 [32, 3072], P(('section', 'dp')), may hold values from 0 to 35, never falling along the last dimension, each value on 1 to 256 neighbouring positions
- out_weight: bfloat16 [1280, 1280], replicated, may hold values from -0.15625 to 0.15625
- cotangent: bfloat16 [32, 3072, 1280], P(('section', 'dp'), 'seq'), may hold values from -6 to 6
Outputs:
- mixed_out: bfloat16 [32, 3072, 1280], P(('section', 'dp'), 'seq')
- weight_grad: float32 [1280, 1280], P(('section', 'dp'))
The draws below stay inside these ranges and needn't reach their ends.
Inputs may be any that keep to these rules, and one draw needn't show every extreme that they name: queries and key_input lie within -5 to 5.
All inputs are finite; a program needn't handle non-finite values.
Results may differ from the reference program's by a relative error of at most 0.015.
Values may be sent and summed in bfloat16 or wider, within the bound.
No kernel may reach another device: no remote copies, remote signals or barrier semaphores. Data moves between devices by JAX's collectives and lax.ppermute only.
A program may use at most 32 MiB of HBM per device.

```python
import math
import jax
import jax.numpy as jnp
import numpy as np
from jax import lax

HEADS = 16
HEAD_DIM = 80
P_DEV = 128
WIDTH = 1280
MOST = 256
SEQ = 3072
SAMPLES = 32
SEGS = 36
N_SEQ = 24


def draw_both(key):
    shape = (SAMPLES, SEQ, HEADS * HEAD_DIM)
    key_query, key_keys = jax.random.split(jax.random.fold_in(key, 4177), 2)
    query_draw = jnp.clip(jax.random.normal(key_query, shape, jnp.float32), -4.0, 4.0)
    keys_draw = jnp.clip(jax.random.normal(key_keys, shape, jnp.float32), -4.0, 4.0)
    return (query_draw, keys_draw)


def draw_queries(key, part):
    return draw_both(key)[0].astype(jnp.bfloat16)


def draw_key_input(key, part):
    return draw_both(key)[1].astype(jnp.bfloat16)


def strengthened(values, own_key, source, target, parts, factor):
    def block_of(axis_at):
        return (jnp.arange(values.shape[axis_at]) // (values.shape[axis_at] // parts)).reshape((-1,) + (1,) * (values.ndim - 1 - axis_at))

    first = jax.random.permutation(own_key, parts)[block_of(target)]
    second = (block_of(target) + parts // 2) % parts
    return jnp.where((block_of(source) == first) | (block_of(source) == second), factor * values, values)


def block_levels(rng, shape, pieces, smallest, high):
    gain = 1.0
    for dim, shards_of in pieces:
        steps = jax.random.uniform(jax.random.fold_in(jax.random.fold_in(rng, 6), dim), (shards_of,), jnp.float32, smallest / len(pieces), high / len(pieces))
        gain = gain * jnp.repeat(jnp.exp(steps), shape[dim] // shards_of).reshape((-1,) + (1,) * (len(shape) - 1 - dim))
    return gain


def length_profile(amount, total, limit, slope):
    loads = [(1 << 20) // math.isqrt(grade ** slope) + 1 for grade in range(2, amount + 1)]
    rest, counts = total - limit - (amount - 1), [1] * (amount - 1)
    while rest > 0:
        movable = [i for i in range(amount - 1) if counts[i] < limit]
        pool, remaining = sum([loads[i] for i in movable]), rest
        for i in movable:
            extra = min(limit - counts[i], max(1, remaining * loads[i] // pool), rest)
            counts[i] = counts[i] + extra
            rest = rest - extra
    return np.array([limit] + counts)


def uneven(key, number_of, total, most, slope):
    if number_of == 2:
        one = jax.random.randint(key, (), max(1, total - most), min(most, total - 1) + 1)
        return jnp.stack([one, total - one])
    sizes = jnp.asarray(length_profile(number_of, total, most, slope), jnp.int32)
    twos = (number_of - 1) // 2
    giver, taker = sizes[1:1 + 2 * twos:2], sizes[2:2 + 2 * twos:2]
    room = jnp.minimum(giver - 1, most - taker)
    passed = jax.random.randint(jax.random.fold_in(key, 1), (twos,), 0, 1 << 20) % (room + 1)
    sizes = sizes.at[1:1 + 2 * twos:2].set(giver - passed).at[2:2 + 2 * twos:2].set(taker + passed)
    return sizes[jax.random.permutation(jax.random.fold_in(key, 2), number_of)]


def noise(rng, shape, scale, most, cuts=(), kind=jnp.bfloat16):
    gain = block_levels(rng, shape, cuts, -0.22, 0.18) if cuts else 1.0
    array = jax.random.normal(rng, shape, jnp.float32) * scale * gain
    return jnp.minimum(jnp.maximum(array, -most), most).astype(kind)


def heavy_noise(key, shape, width, most, shards, heavy, held_as=jnp.bfloat16):
    values = width * jax.random.normal(key, shape, jnp.float32)
    if shards:
        values = values * block_levels(key, shape, shards, -0.22, 0.18)
    return jnp.clip(strengthened(values, jax.random.fold_in(key, 3), *heavy), -most, most).astype(held_as)


def setup_inputs(seed: int = 0) -> dict:
    key_of = jax.random.split(jax.random.key(seed), 8)
    queries = draw_queries(jax.random.fold_in(key_of[7], 71), 0)
    key_input = draw_key_input(jax.random.fold_in(key_of[7], 71), 0)
    value_input = noise(key_of[2], (SAMPLES, SEQ, WIDTH), 1.0, 6.0, ((0, 32), (1, 24)))
    residual = noise(key_of[3], (SAMPLES, SEQ, WIDTH), 0.5, 4.0, ((0, 32), (1, 24)))
    segments = jax.vmap(lambda own: jnp.searchsorted(jnp.cumsum(uneven(own, SEGS, SEQ, MOST, 2)), jnp.arange(SEQ), side="right"))(jax.random.split(key_of[4], SAMPLES)).reshape((SAMPLES, SEQ)).astype(jnp.int32)
    out_weight = noise(key_of[5], (WIDTH, WIDTH), WIDTH ** -0.5, 0.15625)
    cotangent = heavy_noise(key_of[6], (SAMPLES, SEQ, WIDTH), 1.0, 6.0, ((0, 32), (1, 24)), (0, 2, 32, 2.75))
    return dict(queries=queries, key_input=key_input, value_input=value_input, residual=residual, segments=segments, out_weight=out_weight, cotangent=cotangent)


def attend_sample(inputs):
    query_rows, key_rows, value_rows, image_ids = inputs
    margin = MOST
    key_padded = jnp.pad(key_rows, ((margin, margin), (0, 0)))
    value_padded = jnp.pad(value_rows, ((margin, margin), (0, 0)))
    ids_padded = jnp.pad(image_ids, (margin, margin), constant_values=-1)
    span = P_DEV + 2 * margin

    def one_block(block):
        start = (block * P_DEV).astype(jnp.int32)
        query_block = lax.dynamic_slice_in_dim(query_rows, start, P_DEV, 0).astype(jnp.float32)
        query_ids = lax.dynamic_slice_in_dim(image_ids, start, P_DEV, 0)
        key_block = lax.dynamic_slice_in_dim(key_padded, start, span, 0).astype(jnp.float32)
        value_block = lax.dynamic_slice_in_dim(value_padded, start, span, 0).astype(jnp.float32)
        key_ids = lax.dynamic_slice_in_dim(ids_padded, start, span, 0)
        query_heads = query_block.reshape(P_DEV, HEADS, HEAD_DIM)
        key_heads = key_block.reshape(span, HEADS, HEAD_DIM)
        value_heads = value_block.reshape(span, HEADS, HEAD_DIM)
        scores = jnp.einsum("qhd,khd->hqk", query_heads, key_heads) * (HEAD_DIM ** -0.5)
        usable = query_ids[:, None] == key_ids[None, :]
        scores = jnp.where(usable[None], scores, jnp.float32(-1e30))
        highest = jnp.max(scores, axis=-1, keepdims=True)
        expo = jnp.where(usable[None], jnp.exp(scores - highest), jnp.float32(0.0))
        probs = (expo / jnp.sum(expo, axis=-1, keepdims=True)).astype(jnp.bfloat16)
        attended = jnp.einsum("hqk,khd->qhd", probs.astype(jnp.float32), value_heads)
        return attended.reshape(P_DEV, HEADS * HEAD_DIM).astype(jnp.bfloat16)

    result = lax.map(one_block, jnp.arange(N_SEQ, dtype=jnp.int32))
    return result.reshape(SEQ, HEADS * HEAD_DIM)


def reference(queries, key_input, value_input, residual, segments, out_weight, cotangent):
    attended = lax.map(attend_sample, (queries, key_input, value_input, segments))
    projected = lax.dot_general(attended, out_weight, (((2,), (1,)), ((), ())), preferred_element_type=jnp.float32)
    mixed_out = (residual.astype(jnp.float32) + projected).astype(jnp.bfloat16)
    grad_scale = 1.0 / (float(SAMPLES * SEQ) ** 0.5)
    width_all = HEADS * HEAD_DIM

    def add_sample(total, inputs):
        attended_rows, grad_rows = inputs
        attended_blocks = attended_rows.reshape(N_SEQ, P_DEV, width_all).astype(jnp.float32)
        grad_blocks = grad_rows.reshape(N_SEQ, P_DEV, width_all).astype(jnp.float32)
        partial_value = (jnp.einsum("jpo,jpi->joi", grad_blocks, attended_blocks) * grad_scale).astype(jnp.bfloat16)
        return total + jnp.sum(partial_value.astype(jnp.float32), axis=0), None

    weight_grad, _ = lax.scan(add_sample, jnp.zeros((width_all, width_all), jnp.float32), (attended, cotangent))
    return mixed_out, weight_grad
```

```python
import functools

import jax
import jax.numpy as jnp
from jax import lax
from jax.experimental import pallas as pl
from jax.experimental.pallas import tpu as pltpu
from jax.sharding import PartitionSpec as P


HEADS = 16
LOG2E = 1.4426950408889634
AXES = ("section", "seq", "dp")
ANY = pl.BlockSpec(memory_space=pl.ANY)
VMEM = pl.BlockSpec(memory_space=pltpu.VMEM)
SMEM = pl.BlockSpec(memory_space=pltpu.SMEM)
NT = (((1,), (1,)), ((), ()))


def moved(value, target):
    sections, seqs, cores = (lax.axis_size(axis) for axis in AXES)
    pairs = []
    for section in range(sections):
        for seq in range(seqs):
            for core in range(cores):
                to_seq, to_core = target(seq, core)
                if 0 <= to_seq < seqs:
                    source = (section * seqs + seq) * cores + core
                    pairs.append((source, (section * seqs + to_seq) * cores + to_core))
    return lax.ppermute(value, AXES, pairs)


def to_pair(value):
    return moved(value, lambda seq, core: (seq ^ 1, core))


def to_core(value):
    return moved(value, lambda seq, core: (seq, 1 - core))


def to_next(value):
    return moved(value, lambda seq, core: (seq + 2, core))


def to_previous(value):
    return moved(value, lambda seq, core: (seq - 2, core))


def position(place):
    index = place[0]
    return index >> 2, (index >> 1) & 1, index & 1


def split_kernel(
    width, place, query, key, value, cotangent, kv_own, kv_other, q_own, q_other, exchanged
):
    _, y, _ = position(place)
    half = q_own.shape[1]
    own = pl.ds(pl.multiple_of(y * half, half), half)
    other = pl.ds(pl.multiple_of((1 - y) * half, half), half)
    kv_own[0] = key[:, own]
    kv_own[1] = value[:, own]
    kv_other[0] = key[:, other]
    kv_other[1] = value[:, other]
    q_own[...] = query[:, own]
    q_other[...] = query[:, other]
    picked = half // 2
    shift = 20
    factor = -(-(1 << shift) // width)
    assert all((j * factor) >> shift == j // width for j in range(picked))
    row = lax.broadcasted_iota(jnp.int32, (picked, half), 0)
    column = lax.broadcasted_iota(jnp.int32, (picked, half), 1)
    base = row + lax.shift_right_logical(row * factor, shift) * width
    for to_core_index in range(2):
        chosen = (column == base + to_core_index * width).astype(jnp.float32)
        chosen = chosen.astype(jnp.bfloat16)
        parts = [
            lax.dot_general(
                cotangent[:, part * half : (part + 1) * half],
                chosen,
                NT,
                preferred_element_type=jnp.float32,
            )
            for part in range(2)
        ]
        block = jnp.concatenate(parts, axis=1).astype(jnp.bfloat16)
        for side in range(2):
            exchanged[side * 2 + to_core_index] = block


def attention_kernel(
    head_dim, place, segments, q_own, q_pair, kv_own, kv_pair, kv_left, kv_left_pair,
    kv_right, kv_right_pair, attended, passed, queries, keys, values, bias, mixed, sems
):
    rows, half = q_own.shape
    total = segments.shape[1]
    z, y, _ = position(place)
    blocks = (kv_own, kv_pair, kv_left, kv_left_pair, kv_right, kv_right_pair)
    copies = [
        pltpu.make_async_copy(q_own, queries.at[pl.ds(0, rows)], sems.at[0]),
        pltpu.make_async_copy(q_pair, queries.at[pl.ds(rows, rows)], sems.at[1]),
    ]
    for i, block in enumerate(blocks):
        here = pl.ds(i * rows, rows)
        copies.append(pltpu.make_async_copy(block.at[0], keys.at[here], sems.at[2 + 2 * i]))
        copies.append(pltpu.make_async_copy(block.at[1], values.at[here], sems.at[3 + 2 * i]))
    for copy in copies:
        copy.start()
    ids = []
    for unit in (0, -1, 1):
        for side in (y, 1 - y):
            offset = ((z + unit) * 2 + side) * rows
            start = pl.multiple_of(jnp.clip(offset, 0, total - rows), rows)
            row = segments[:, pl.ds(start, rows)]
            ids.append(jnp.where((offset >= 0) & (offset < total), row, -1))
    for i in range(2):
        query_ids = jnp.transpose(jnp.broadcast_to(ids[i], (rows, rows)))
        for j in range(6):
            bias[i * rows : (i + 1) * rows, j * rows : (j + 1) * rows] = jnp.where(
                query_ids == ids[j], jnp.float32(0.0), jnp.float32(-1e30)
            )
    mixed[...] = jnp.zeros_like(mixed)
    for copy in copies:
        copy.wait()
    scale = head_dim ** (-0.5) * LOG2E
    for i in range(2):
        here = slice(i * rows, (i + 1) * rows)
        for head in range(half // head_dim):
            first, last = head * head_dim, (head + 1) * head_dim
            low, high = first // 128 * 128, -(-last // 128) * 128
            lane = lax.broadcasted_iota(jnp.int32, (rows, high - low), 1) + low
            inside = (lane >= first) & (lane < last)
            query = jnp.where(inside, queries[here, low:high], jnp.zeros((), jnp.bfloat16))
            scores = lax.dot_general(
                query, keys[:, low:high], NT, preferred_element_type=jnp.float32
            )
            scores = scores + bias[here, :]
            highest = jnp.max(scores, axis=-1, keepdims=True)
            expo = jnp.exp2((scores - highest) * scale)
            norm = 1.0 / jnp.sum(expo, axis=-1, keepdims=True)
            weighted = jnp.dot(
                expo.astype(jnp.bfloat16), values[:, low:high], preferred_element_type=jnp.float32
            )
            mixed[here, low:high] = jnp.where(inside, weighted * norm, mixed[here, low:high])
    attended[...] = mixed[...].astype(jnp.bfloat16)
    passed[...] = mixed[rows:, :].astype(jnp.bfloat16)


def gradient_kernel(share, width, place, att, att_core, exchanged, out):
    _, y, core = position(place)
    order = (2 * y + core, 2 * (1 - y) + core, 2 * y + 1 - core, 2 * (1 - y) + 1 - core)
    left = jnp.concatenate([exchanged[index] for index in order], axis=0)
    right = jnp.concatenate([att[...], att_core[...]], axis=0)
    full = lax.dot_general(
        left, right, (((0,), (0,)), ((), ())), preferred_element_type=jnp.float32
    )
    wide = full.shape[1] // 128
    parts = out.shape[0] // (full.shape[0] // width)
    for section in range(full.shape[0] // width):
        for part in range(parts):
            for slot in range(share):
                row, column = divmod(part * share + slot, wide)
                if row * 8 < width:
                    row = section * width + row * 8
                    tile = full[row : row + 8, column * 128 : (column + 1) * 128]
                else:
                    tile = jnp.zeros((8, 128), jnp.float32)
                out[section * parts + part, slot * 8 : (slot + 1) * 8, :] = tile.astype(
                    jnp.bfloat16
                )


def total_kernel(scale, terms, out):
    total = jnp.sum(terms[...].astype(jnp.float32), axis=0) * scale
    total = total.astype(jnp.bfloat16)
    for i in range(out.shape[0]):
        out[i] = total


def assembly_kernel(share, parts, terms, out):
    groups = terms.shape[0] // (2 * parts)
    wide = out.shape[1] // 256
    for side in range(2):
        for tile in range(out.shape[0] // 8 * wide):
            row, column = divmod(tile, wide)
            part, slot = divmod(tile, share)
            total = sum(
                terms[(group * parts + part) * 2 + side, slot * 8 : (slot + 1) * 8, :].astype(
                    jnp.float32
                )
                for group in range(groups)
            )
            column = (side * wide + column) * 128
            out[row * 8 : (row + 1) * 8, column : column + 128] = total


def projection_kernel(place, attended, received, weight, residual, out):
    rows, half = received.shape
    _, y, _ = position(place)
    own = pl.ds(pl.multiple_of(y * half, half), half)
    other = pl.ds(pl.multiple_of((1 - y) * half, half), half)
    total = lax.dot_general(
        attended[:rows, :], weight[:, own], NT, preferred_element_type=jnp.float32
    )
    total += lax.dot_general(
        received[...], weight[:, other], NT, preferred_element_type=jnp.float32
    )
    out[...] = (residual[...].astype(jnp.float32) + total).astype(jnp.bfloat16)


def call(kernel, outs, in_specs, flops, moved_bytes, scratch=(), grant=16):
    return pl.pallas_call(
        kernel,
        out_shape=outs,
        in_specs=in_specs,
        out_specs=jax.tree.map(lambda _: VMEM, outs),
        scratch_shapes=scratch,
        cost_estimate=pl.CostEstimate(
            flops=flops, bytes_accessed=moved_bytes, transcendentals=0
        ),
        compiler_params=pltpu.CompilerParams(vmem_limit_bytes=grant << 20),
    )


def per_device(queries, key_input, value_input, residual, segments, out_weight, cotangent):
    rows, features = queries.shape[1], queries.shape[2]
    half = features // 2
    head_dim = features // HEADS
    sections, seqs, cores = (lax.axis_size(axis) for axis in AXES)
    units = seqs // 2
    width = features // (sections * cores)
    place = lax.axis_index(("seq", "dp")).astype(jnp.int32).reshape(1)

    def bf16(*shape):
        return jax.ShapeDtypeStruct(shape, jnp.bfloat16)

    kv_own, kv_other, q_own, q_other, exchanged = call(
        functools.partial(split_kernel, width),
        (
            bf16(2, rows, half),
            bf16(2, rows, half),
            bf16(rows, half),
            bf16(rows, half),
            bf16(4, rows, half),
        ),
        [SMEM, VMEM, VMEM, VMEM, VMEM],
        2 * half * features * rows,
        24 * rows * features,
        grant=62,
    )(place, queries[0], key_input[0], value_input[0], cotangent[0])
    kv_pair = to_pair(kv_other)
    kv_left = to_next(kv_own)
    kv_right = to_previous(kv_own)
    kv_left_pair = to_next(kv_pair)
    kv_right_pair = to_previous(kv_pair)
    q_pair = to_pair(q_other)
    quads = [list(range(first, first + 4)) for first in range(0, 2 * seqs, 4)]
    exchanged = lax.all_to_all(exchanged, ("seq", "dp"), 0, 0, tiled=True, axis_index_groups=quads)
    attended, passed = call(
        functools.partial(attention_kernel, head_dim),
        (bf16(2 * rows, half), bf16(rows, half)),
        [SMEM, VMEM] + [ANY] * 8,
        4 * 2 * rows * 6 * rows * half,
        26 * rows * half,
        scratch=[
            pltpu.VMEM((2 * rows, half), jnp.bfloat16),
            pltpu.VMEM((6 * rows, half), jnp.bfloat16),
            pltpu.VMEM((6 * rows, half), jnp.bfloat16),
            pltpu.VMEM((2 * rows, 6 * rows), jnp.float32),
            pltpu.VMEM((2 * rows, half), jnp.float32),
            pltpu.SemaphoreType.DMA((14,)),
        ],
    )(
        place, segments, q_own, q_pair, kv_own, kv_pair, kv_left, kv_left_pair,
        kv_right, kv_right_pair,
    )
    attended_core = to_core(attended)
    received = to_pair(passed)
    parts = 4 if units % 4 == 0 else 2
    tiles = width // 8 * (half // 128)
    share = -(-tiles // parts)
    partial = call(
        functools.partial(gradient_kernel, share, width),
        bf16(sections * parts, share * 8, 128),
        [SMEM, VMEM, VMEM, VMEM],
        2 * half * half * 4 * rows,
        2 * half * half,
    )(place, attended, attended_core, exchanged)
    mixed_out = call(
        projection_kernel,
        bf16(rows, features),
        [SMEM] + [VMEM] * 4,
        2 * rows * features * features,
        2 * features * features,
    )(place, attended, received, out_weight, residual[0])

    groups = sections * cores
    grad_scale = 1.0 / float(groups * seqs * rows) ** 0.5
    cubes = [
        [
            (section * seqs + (first + part) * 2 + side) * cores + core
            for section in range(sections)
            for part in range(parts)
        ]
        for first in range(0, units, parts)
        for side in range(2)
        for core in range(cores)
    ]
    terms = lax.all_to_all(partial, AXES, 0, 0, tiled=True, axis_index_groups=cubes)
    spread = call(
        functools.partial(total_kernel, grad_scale),
        bf16(seqs, share * 8, 128),
        [VMEM],
        sections * parts * share * 1024,
        2 * (sections * parts + seqs) * share * 1024,
    )(terms)
    spread = lax.all_to_all(spread, "seq", 0, 0, tiled=True)
    weight_grad = call(
        functools.partial(assembly_kernel, share, parts),
        jax.ShapeDtypeStruct((width, features), jnp.float32),
        [VMEM],
        seqs * share * 1024,
        2 * seqs * share * 1024,
    )(spread)
    return (mixed_out[None], weight_grad)


def solution(mesh):
    in_specs = (
        P(("section", "dp"), "seq", None),
        P(("section", "dp"), "seq", None),
        P(("section", "dp"), "seq", None),
        P(("section", "dp"), "seq", None),
        P(("section", "dp"), None),
        P(),
        P(("section", "dp"), "seq", None),
    )
    out_specs = (P(("section", "dp"), "seq", None), P(("section", "dp"), None))
    return jax.shard_map(
        per_device, mesh=mesh, in_specs=in_specs, out_specs=out_specs, check_vma=False
    )
```

```python
import functools

import jax
import jax.numpy as jnp
from jax import lax
from jax.experimental import pallas as pl
from jax.experimental.pallas import tpu as pltpu
from jax.sharding import PartitionSpec as P


HEADS = 16
LOG2E = 1.4426950408889634
AXES = ("section", "seq", "dp")
ANY = pl.BlockSpec(memory_space=pl.ANY)
HBM = pl.BlockSpec(memory_space=pltpu.HBM)
VMEM = pl.BlockSpec(memory_space=pltpu.VMEM)
SMEM = pl.BlockSpec(memory_space=pltpu.SMEM)
NT = (((1,), (1,)), ((), ()))
TT = (((0,), (1,)), ((), ()))


def moved(value, target):
    sections, seqs, cores = (lax.axis_size(axis) for axis in AXES)
    pairs = []
    for section in range(sections):
        for seq in range(seqs):
            for core in range(cores):
                to_seq, to_core = target(seq, core)
                if 0 <= to_seq < seqs:
                    source = (section * seqs + seq) * cores + core
                    pairs.append((source, (section * seqs + to_seq) * cores + to_core))
    return lax.ppermute(value, AXES, pairs)


def to_pair(value):
    return moved(value, lambda seq, core: (seq ^ 1, core))


def to_core(value):
    return moved(value, lambda seq, core: (seq, 1 - core))


def to_next(value):
    return moved(value, lambda seq, core: (seq + 2, core))


def to_previous(value):
    return moved(value, lambda seq, core: (seq - 2, core))


def position(place):
    index = place[0]
    return index >> 2, (index >> 1) & 1, index & 1


def split_kernel(
    width, place, query, key, value, cotangent, kv_own, kv_other, q_own, q_other, exchanged
):
    _, y, _ = position(place)
    half = q_own.shape[1]
    own = pl.ds(pl.multiple_of(y * half, half), half)
    other = pl.ds(pl.multiple_of((1 - y) * half, half), half)
    for part, out in ((own, kv_own), (other, kv_other)):
        out[0] = key[:, part]
        chosen = value[:, part]
        for first in range(0, half, 128):
            out[1, :, first : first + 128] = jnp.transpose(chosen[:, first : first + 128])
    q_own[...] = query[:, own]
    q_other[...] = query[:, other]
    picked = half // 2
    shift = 20
    factor = -(-(1 << shift) // width)
    assert all((j * factor) >> shift == j // width for j in range(picked))
    row = lax.broadcasted_iota(jnp.int32, (picked, half), 0)
    column = lax.broadcasted_iota(jnp.int32, (picked, half), 1)
    base = row + lax.shift_right_logical(row * factor, shift) * width
    for to_core_index in range(2):
        chosen = (column == base + to_core_index * width).astype(jnp.float32)
        chosen = chosen.astype(jnp.bfloat16)
        for part in range(2):
            block = lax.dot_general(
                chosen,
                cotangent[:, part * half : (part + 1) * half],
                NT,
                preferred_element_type=jnp.float32,
            ).astype(jnp.bfloat16)
            for side in range(2):
                exchanged[
                    side * 2 + to_core_index, part * picked : (part + 1) * picked, :
                ] = block


def attention_kernel(
    head_dim, place, segments, q_own, q_pair, kv_own, kv_pair, kv_left, kv_left_pair,
    kv_right, kv_right_pair, attended, passed, queries, keys, values, bias, scores, probs, sems
):
    rows, half = q_own.shape
    total = segments.shape[1]
    heads = half // head_dim
    z, y, _ = position(place)
    blocks = (kv_own, kv_pair, kv_left, kv_left_pair, kv_right, kv_right_pair)
    moves = [(q_own, queries.at[pl.ds(0, rows)]), (q_pair, queries.at[pl.ds(rows, rows)])]
    for i, block in enumerate(blocks):
        here = pl.ds(i * rows, rows)
        moves.append((block.at[0], keys.at[here]))
        for first in range(0, half, 128):
            some = pl.ds(first, 128)
            moves.append((block.at[1, :, some], values.at[some, here]))
    copies = [
        pltpu.make_async_copy(source, target, sems.at[i])
        for i, (source, target) in enumerate(moves)
    ]
    for copy in copies:
        copy.start()
    ids = []
    for i in range(6):
        offset = ((z + (0, -1, 1)[i // 2]) * 2 + (y if i % 2 == 0 else 1 - y)) * rows
        start = pl.multiple_of(jnp.clip(offset, 0, total - rows), rows)
        row = segments[:, pl.ds(start, rows)]
        ids.append(jnp.where((offset >= 0) & (offset < total), row, -1))
    for i in range(6):
        key_ids = jnp.transpose(jnp.broadcast_to(ids[i], (rows, rows)))
        for j in range(2):
            bias[i * rows : (i + 1) * rows, j * rows : (j + 1) * rows] = jnp.where(
                key_ids == ids[j], jnp.float32(0.0), jnp.float32(-1e30)
            )
    for copy in copies:
        copy.wait()
    scale = head_dim ** (-0.5) * LOG2E
    ones = jnp.ones((16, 6 * rows), jnp.bfloat16)
    step = 64

    def multiply(head):
        first, last = head * head_dim, (head + 1) * head_dim
        low, high = first // 128 * 128, -(-last // 128) * 128
        lane = lax.broadcasted_iota(jnp.int32, (2 * rows, high - low), 1) + low
        inside = (lane >= first) & (lane < last)
        query = jnp.where(inside, queries[:, low:high], jnp.zeros((), jnp.bfloat16))
        found = lax.dot_general(
            keys[:, low:high], query, NT, preferred_element_type=jnp.float32
        )
        found = found + bias[...]
        scores[head % 2] = found
        return jnp.max(found, axis=0, keepdims=True)

    highest = multiply(0)
    for head in range(heads):
        following = multiply(head + 1) if head + 1 < heads else None
        for low in range(0, 6 * rows, step):
            some = slice(low, low + step)
            expo = jnp.exp2((scores[head % 2, some, :] - highest) * scale)
            probs[head % 2, some, :] = expo.astype(jnp.bfloat16)
        here = slice(head * head_dim, (head + 1) * head_dim)
        weighted = jnp.dot(
            jnp.concatenate([values[here, :], ones], axis=0),
            probs[head % 2],
            preferred_element_type=jnp.float32,
        )
        norm = 1.0 / weighted[head_dim : head_dim + 1, :]
        result = (weighted[:head_dim, :] * norm).astype(jnp.bfloat16)
        attended[here, :] = result
        passed[here, :] = result[:, rows:]
        highest = following


def gradient_kernel(place, att, att_core, exchanged, out):
    _, y, core = position(place)
    order = (2 * y + core, 2 * (1 - y) + core, 2 * y + 1 - core, 2 * (1 - y) + 1 - core)
    left = jnp.concatenate([exchanged[index] for index in order], axis=1)
    right = jnp.concatenate([att[...], att_core[...]], axis=1)
    out[...] = lax.dot_general(left, right, NT, preferred_element_type=jnp.float32).astype(
        jnp.bfloat16
    )


def first_sum_kernel(width, terms, out):
    parts = out.shape[0] // (terms.shape[1] // width)
    tall = out.shape[1]
    for block in range(terms.shape[1] // width):
        some = slice(block * width, (block + 1) * width)
        total = sum(terms[i, some, :].astype(jnp.float32) for i in range(terms.shape[0]))
        for part in range(parts):
            column, row = part // 2 * 128, part % 2 * tall
            if column < terms.shape[2]:
                tile = total[row : row + tall, column : column + 128]
                if tile.shape[0] < tall:
                    tile = jnp.concatenate(
                        [tile, jnp.zeros((tall - tile.shape[0], 128), jnp.float32)], axis=0
                    )
            else:
                tile = jnp.zeros((tall, 128), jnp.float32)
            out[block * parts + part] = tile.astype(jnp.bfloat16)


def second_sum_kernel(scale, terms, out):
    total = sum(terms[i].astype(jnp.float32) for i in range(terms.shape[0])) * scale
    total = total.astype(jnp.bfloat16)
    for i in range(out.shape[0]):
        out[i] = total


def assembly_kernel(terms, out):
    width, features = out.shape
    tall = terms.shape[1]
    for side in range(2):
        for part in range(features // 128):
            row = part % 2 * tall
            rows = min(tall, width - row)
            column = side * (features // 2) + part // 2 * 128
            tile = terms[part * 2 + side].astype(jnp.float32)
            out[row : row + rows, column : column + 128] = tile[:rows, :]


def projection_kernel(place, attended, received, weight, residual, out):
    half, rows = received.shape
    _, y, _ = position(place)
    own = pl.ds(pl.multiple_of(y * half, half), half)
    other = pl.ds(pl.multiple_of((1 - y) * half, half), half)
    total = lax.dot_general(
        attended[:, :rows], weight[:, own], TT, preferred_element_type=jnp.float32
    )
    total += lax.dot_general(
        received[...], weight[:, other], TT, preferred_element_type=jnp.float32
    )
    out[...] = (residual[...].astype(jnp.float32) + total).astype(jnp.bfloat16)


def call(kernel, outs, in_specs, flops, moved_bytes, scratch=(), grant=16):
    return pl.pallas_call(
        kernel,
        out_shape=outs,
        in_specs=in_specs,
        out_specs=jax.tree.map(lambda _: VMEM, outs),
        scratch_shapes=scratch,
        cost_estimate=pl.CostEstimate(
            flops=flops, bytes_accessed=moved_bytes, transcendentals=0
        ),
        compiler_params=pltpu.CompilerParams(vmem_limit_bytes=grant << 20),
    )


def per_device(queries, key_input, value_input, residual, segments, out_weight, cotangent):
    rows, features = queries.shape[1], queries.shape[2]
    half = features // 2
    head_dim = features // HEADS
    sections, seqs, cores = (lax.axis_size(axis) for axis in AXES)
    units = seqs // 2
    width = features // (sections * cores)
    place = lax.axis_index(("seq", "dp")).astype(jnp.int32).reshape(1)

    def bf16(*shape):
        return jax.ShapeDtypeStruct(shape, jnp.bfloat16)

    kv_own, kv_other, q_own, q_other, exchanged = call(
        functools.partial(split_kernel, width),
        (
            bf16(2, rows, half),
            bf16(2, rows, half),
            bf16(rows, half),
            bf16(rows, half),
            bf16(4, half, rows),
        ),
        [SMEM, VMEM, VMEM, VMEM, VMEM],
        2 * half * features * rows,
        24 * rows * features,
        grant=62,
    )(place, queries[0], key_input[0], value_input[0], cotangent[0])
    kv_pair = to_pair(kv_other)
    kv_left = to_next(kv_own)
    kv_right = to_previous(kv_own)
    kv_left_pair = to_next(kv_pair)
    kv_right_pair = to_previous(kv_pair)
    q_pair = to_pair(q_other)
    quads = [list(range(first, first + 4)) for first in range(0, 2 * seqs, 4)]
    exchanged = lax.all_to_all(exchanged, ("seq", "dp"), 0, 0, tiled=True, axis_index_groups=quads)
    attended, passed = call(
        functools.partial(attention_kernel, head_dim),
        (bf16(half, 2 * rows), bf16(half, rows)),
        [SMEM, VMEM] + [ANY] * 8,
        4 * 2 * rows * 6 * rows * half,
        26 * rows * half,
        scratch=[
            pltpu.VMEM((2 * rows, half), jnp.bfloat16),
            pltpu.VMEM((6 * rows, half), jnp.bfloat16),
            pltpu.VMEM((half, 6 * rows), jnp.bfloat16),
            pltpu.VMEM((6 * rows, 2 * rows), jnp.float32),
            pltpu.VMEM((2, 6 * rows, 2 * rows), jnp.float32),
            pltpu.VMEM((2, 6 * rows, 2 * rows), jnp.bfloat16),
            pltpu.SemaphoreType.DMA((2 + 6 * (1 + half // 128),)),
        ],
        grant=16,
    )(
        place, segments, q_own, q_pair, kv_own, kv_pair, kv_left, kv_left_pair,
        kv_right, kv_right_pair,
    )
    attended_core = to_core(attended)
    received = to_pair(passed)
    partial = call(
        gradient_kernel,
        bf16(half, half),
        [SMEM, VMEM, VMEM, VMEM],
        2 * half * half * 4 * rows,
        2 * half * half,
        grant=62,
    )(place, attended, attended_core, exchanged)
    mixed_out = call(
        projection_kernel,
        bf16(rows, features),
        [SMEM] + [VMEM] * 4,
        2 * rows * features * features,
        2 * features * features,
        grant=16,
    )(place, attended, received, out_weight, residual[0])

    groups = sections * cores
    grad_scale = 1.0 / float(groups * seqs * rows) ** 0.5
    side_x, side_y = 4, sections // 4
    parts, tall = units, 24
    lines = [
        [(x * side_y + y) for x in range(side_x)] for y in range(side_y)
    ]
    terms = lax.all_to_all(
        partial.reshape(side_x, side_y * width, half),
        "section",
        0,
        0,
        tiled=True,
        axis_index_groups=lines,
    )
    terms = call(
        functools.partial(first_sum_kernel, width),
        bf16(side_y * parts, tall, 128),
        [VMEM],
        half * half,
        3 * half * half,
    )(terms)
    planes = [
        [
            ((x * side_y + y) * seqs + (first + part) * 2 + side) * cores + core
            for y in range(side_y)
            for part in range(parts)
        ]
        for x in range(side_x)
        for first in range(0, units, parts)
        for side in range(2)
        for core in range(cores)
    ]
    terms = lax.all_to_all(terms, AXES, 0, 0, tiled=True, axis_index_groups=planes)
    spread = call(
        functools.partial(second_sum_kernel, grad_scale),
        bf16(seqs, tall, 128),
        [VMEM],
        side_y * parts * tall * 128,
        2 * (side_y * parts + seqs) * tall * 128,
    )(terms)
    spread = lax.all_to_all(spread, "seq", 0, 0, tiled=True)
    weight_grad = call(
        assembly_kernel,
        jax.ShapeDtypeStruct((width, features), jnp.float32),
        [VMEM],
        seqs * tall * 128,
        2 * seqs * tall * 128,
    )(spread)
    return (mixed_out[None], weight_grad)


def solution(mesh):
    in_specs = (
        P(("section", "dp"), "seq", None),
        P(("section", "dp"), "seq", None),
        P(("section", "dp"), "seq", None),
        P(("section", "dp"), "seq", None),
        P(("section", "dp"), None),
        P(),
        P(("section", "dp"), "seq", None),
    )
    out_specs = (P(("section", "dp"), "seq", None), P(("section", "dp"), None))
    return jax.shard_map(
        per_device, mesh=mesh, in_specs=in_specs, out_specs=out_specs, check_vma=False
    )
```

```python
import functools

import jax
import jax.numpy as jnp
from jax import lax
from jax.experimental import pallas as pl
from jax.experimental.pallas import tpu as pltpu
from jax.sharding import PartitionSpec as P


HEADS = 16
LOG2E = 1.4426950408889634
AXES = ("section", "seq", "dp")
ANY = pl.BlockSpec(memory_space=pl.ANY)
HBM = pl.BlockSpec(memory_space=pltpu.HBM)
VMEM = pl.BlockSpec(memory_space=pltpu.VMEM)
SMEM = pl.BlockSpec(memory_space=pltpu.SMEM)
NT = (((1,), (1,)), ((), ()))
TT = (((0,), (1,)), ((), ()))


def moved(value, target):
    sections, seqs, cores = (lax.axis_size(axis) for axis in AXES)
    pairs = []
    for section in range(sections):
        for seq in range(seqs):
            for core in range(cores):
                to_seq, to_core = target(seq, core)
                if 0 <= to_seq < seqs:
                    source = (section * seqs + seq) * cores + core
                    pairs.append((source, (section * seqs + to_seq) * cores + to_core))
    return lax.ppermute(value, AXES, pairs)


def to_pair(value):
    return moved(value, lambda seq, core: (seq ^ 1, core))


def to_core(value):
    return moved(value, lambda seq, core: (seq, 1 - core))


def to_next(value):
    return moved(value, lambda seq, core: (seq + 2, core))


def to_previous(value):
    return moved(value, lambda seq, core: (seq - 2, core))


def position(place):
    index = place[0]
    return index >> 2, (index >> 1) & 1, index & 1


def split_kernel(
    width, place, query, key, value, cotangent, kv_own, kv_other, q_own, q_other, exchanged
):
    _, y, _ = position(place)
    half = q_own.shape[1]
    own = pl.ds(pl.multiple_of(y * half, half), half)
    other = pl.ds(pl.multiple_of((1 - y) * half, half), half)
    for part, out in ((own, kv_own), (other, kv_other)):
        out[0] = key[:, part]
        chosen = value[:, part]
        for first in range(0, half, 128):
            out[1, :, first : first + 128] = jnp.transpose(chosen[:, first : first + 128])
    q_own[...] = query[:, own]
    q_other[...] = query[:, other]
    picked = half // 2
    shift = 20
    factor = -(-(1 << shift) // width)
    assert all((j * factor) >> shift == j // width for j in range(picked))
    row = lax.broadcasted_iota(jnp.int32, (picked, half), 0)
    column = lax.broadcasted_iota(jnp.int32, (picked, half), 1)
    base = row + lax.shift_right_logical(row * factor, shift) * width
    for to_core_index in range(2):
        chosen = (column == base + to_core_index * width).astype(jnp.float32)
        chosen = chosen.astype(jnp.bfloat16)
        for part in range(2):
            block = lax.dot_general(
                chosen,
                cotangent[:, part * half : (part + 1) * half],
                NT,
                preferred_element_type=jnp.float32,
            ).astype(jnp.bfloat16)
            for side in range(2):
                exchanged[
                    side * 2 + to_core_index, part * picked : (part + 1) * picked, :
                ] = block


def attention_kernel(
    head_dim, place, segments, q_own, q_pair, kv_own, kv_pair, kv_left, kv_left_pair,
    kv_right, kv_right_pair, attended, passed, queries, keys, values, bias, scores, probs, sems
):
    rows, half = q_own.shape
    total = segments.shape[1]
    heads = half // head_dim
    z, y, _ = position(place)
    blocks = (kv_own, kv_pair, kv_left, kv_left_pair, kv_right, kv_right_pair)
    moves = [(q_own, queries.at[pl.ds(0, rows)]), (q_pair, queries.at[pl.ds(rows, rows)])]
    for i, block in enumerate(blocks):
        here = pl.ds(i * rows, rows)
        moves.append((block.at[0], keys.at[here]))
        for first in range(0, half, 128):
            some = pl.ds(first, 128)
            moves.append((block.at[1, :, some], values.at[some, here]))
    copies = [
        pltpu.make_async_copy(source, target, sems.at[i])
        for i, (source, target) in enumerate(moves)
    ]
    for copy in copies:
        copy.start()
    ids = []
    for i in range(6):
        offset = ((z + (0, -1, 1)[i // 2]) * 2 + (y if i % 2 == 0 else 1 - y)) * rows
        start = pl.multiple_of(jnp.clip(offset, 0, total - rows), rows)
        row = segments[:, pl.ds(start, rows)]
        ids.append(jnp.where((offset >= 0) & (offset < total), row, -1))
    for i in range(6):
        key_ids = jnp.transpose(jnp.broadcast_to(ids[i], (rows, rows)))
        for j in range(2):
            bias[i * rows : (i + 1) * rows, j * rows : (j + 1) * rows] = jnp.where(
                key_ids == ids[j], jnp.float32(0.0), jnp.float32(-1e30)
            )
    for copy in copies:
        copy.wait()
    scale = head_dim ** (-0.5) * LOG2E
    ones = jnp.ones((16, 6 * rows), jnp.bfloat16)
    step = 64

    def multiply(head):
        first, last = head * head_dim, (head + 1) * head_dim
        low, high = first // 128 * 128, -(-last // 128) * 128
        lane = lax.broadcasted_iota(jnp.int32, (2 * rows, high - low), 1) + low
        inside = (lane >= first) & (lane < last)
        query = jnp.where(inside, queries[:, low:high], jnp.zeros((), jnp.bfloat16))
        found = lax.dot_general(
            keys[:, low:high], query, NT, preferred_element_type=jnp.float32
        )
        found = found + bias[...]
        scores[head % 2] = found
        return jnp.max(found, axis=0, keepdims=True)

    highest = multiply(0)
    for head in range(heads):
        following = multiply(head + 1) if head + 1 < heads else None
        for low in range(0, 6 * rows, step):
            some = slice(low, low + step)
            expo = jnp.exp2((scores[head % 2, some, :] - highest) * scale)
            probs[head % 2, some, :] = expo.astype(jnp.bfloat16)
        here = slice(head * head_dim, (head + 1) * head_dim)
        weighted = jnp.dot(
            jnp.concatenate([values[here, :], ones], axis=0),
            probs[head % 2],
            preferred_element_type=jnp.float32,
        )
        norm = 1.0 / weighted[head_dim : head_dim + 1, :]
        result = (weighted[:head_dim, :] * norm).astype(jnp.bfloat16)
        attended[here, :] = result
        passed[here, :] = result[:, rows:]
        highest = following


def gradient_kernel(place, att, att_core, exchanged, out):
    _, y, core = position(place)
    order = (2 * y + core, 2 * (1 - y) + core, 2 * y + 1 - core, 2 * (1 - y) + 1 - core)
    left = jnp.concatenate([exchanged[index] for index in order], axis=1)
    right = jnp.concatenate([att[...], att_core[...]], axis=1)
    out[...] = lax.dot_general(left, right, NT, preferred_element_type=jnp.float32).astype(
        jnp.bfloat16
    )


def first_sum_kernel(terms, out):
    out[...] = sum(terms[i].astype(jnp.float32) for i in range(terms.shape[0])).astype(
        jnp.bfloat16
    )


def second_sum_kernel(terms, out):
    total = sum(terms[i].astype(jnp.float32) for i in range(terms.shape[0]))
    tall = out.shape[1]
    for part in range(out.shape[0]):
        column, row = part // 2 * 128, part % 2 * tall
        if column < terms.shape[2]:
            tile = total[row : row + tall, column : column + 128]
            if tile.shape[0] < tall:
                tile = jnp.concatenate(
                    [tile, jnp.zeros((tall - tile.shape[0], 128), jnp.float32)], axis=0
                )
        else:
            tile = jnp.zeros((tall, 128), jnp.float32)
        out[part] = tile.astype(jnp.bfloat16)


def third_sum_kernel(scale, terms, out):
    total = sum(terms[i].astype(jnp.float32) for i in range(terms.shape[0])) * scale
    total = total.astype(jnp.bfloat16)
    for i in range(out.shape[0]):
        out[i] = total


def assembly_kernel(terms, out):
    width, features = out.shape
    tall = terms.shape[1]
    for side in range(2):
        for part in range(features // 128):
            row = part % 2 * tall
            rows = min(tall, width - row)
            column = side * (features // 2) + part // 2 * 128
            tile = terms[part * 2 + side].astype(jnp.float32)
            out[row : row + rows, column : column + 128] = tile[:rows, :]


def projection_kernel(place, attended, received, weight, residual, out):
    half, rows = received.shape
    _, y, _ = position(place)
    own = pl.ds(pl.multiple_of(y * half, half), half)
    other = pl.ds(pl.multiple_of((1 - y) * half, half), half)
    total = lax.dot_general(
        attended[:, :rows], weight[:, own], TT, preferred_element_type=jnp.float32
    )
    total += lax.dot_general(
        received[...], weight[:, other], TT, preferred_element_type=jnp.float32
    )
    out[...] = (residual[...].astype(jnp.float32) + total).astype(jnp.bfloat16)


def call(kernel, outs, in_specs, flops, moved_bytes, scratch=(), grant=16):
    return pl.pallas_call(
        kernel,
        out_shape=outs,
        in_specs=in_specs,
        out_specs=jax.tree.map(lambda _: VMEM, outs),
        scratch_shapes=scratch,
        cost_estimate=pl.CostEstimate(
            flops=flops, bytes_accessed=moved_bytes, transcendentals=0
        ),
        compiler_params=pltpu.CompilerParams(vmem_limit_bytes=grant << 20),
    )


def per_device(queries, key_input, value_input, residual, segments, out_weight, cotangent):
    rows, features = queries.shape[1], queries.shape[2]
    half = features // 2
    head_dim = features // HEADS
    sections, seqs, cores = (lax.axis_size(axis) for axis in AXES)
    units = seqs // 2
    width = features // (sections * cores)
    place = lax.axis_index(("seq", "dp")).astype(jnp.int32).reshape(1)

    def bf16(*shape):
        return jax.ShapeDtypeStruct(shape, jnp.bfloat16)

    kv_own, kv_other, q_own, q_other, exchanged = call(
        functools.partial(split_kernel, width),
        (
            bf16(2, rows, half),
            bf16(2, rows, half),
            bf16(rows, half),
            bf16(rows, half),
            bf16(4, half, rows),
        ),
        [SMEM, VMEM, VMEM, VMEM, VMEM],
        2 * half * features * rows,
        24 * rows * features,
        grant=62,
    )(place, queries[0], key_input[0], value_input[0], cotangent[0])
    kv_pair = to_pair(kv_other)
    kv_left = to_next(kv_own)
    kv_right = to_previous(kv_own)
    kv_left_pair = to_next(kv_pair)
    kv_right_pair = to_previous(kv_pair)
    q_pair = to_pair(q_other)
    quads = [list(range(first, first + 4)) for first in range(0, 2 * seqs, 4)]
    exchanged = lax.all_to_all(
        exchanged, ("seq", "dp"), 0, 0, tiled=True, axis_index_groups=quads
    )
    attended, passed = call(
        functools.partial(attention_kernel, head_dim),
        (bf16(half, 2 * rows), bf16(half, rows)),
        [SMEM, VMEM] + [ANY] * 8,
        4 * 2 * rows * 6 * rows * half,
        26 * rows * half,
        scratch=[
            pltpu.VMEM((2 * rows, half), jnp.bfloat16),
            pltpu.VMEM((6 * rows, half), jnp.bfloat16),
            pltpu.VMEM((half, 6 * rows), jnp.bfloat16),
            pltpu.VMEM((6 * rows, 2 * rows), jnp.float32),
            pltpu.VMEM((2, 6 * rows, 2 * rows), jnp.float32),
            pltpu.VMEM((2, 6 * rows, 2 * rows), jnp.bfloat16),
            pltpu.SemaphoreType.DMA((2 + 6 * (1 + half // 128),)),
        ],
        grant=16,
    )(
        place, segments, q_own, q_pair, kv_own, kv_pair, kv_left, kv_left_pair,
        kv_right, kv_right_pair,
    )
    attended_core = to_core(attended)
    received = to_pair(passed)
    partial = call(
        gradient_kernel,
        bf16(half, half),
        [SMEM, VMEM, VMEM, VMEM],
        2 * half * half * 4 * rows,
        2 * half * half,
        grant=62,
    )(place, attended, attended_core, exchanged)
    mixed_out = call(
        projection_kernel,
        bf16(rows, features),
        [SMEM] + [VMEM] * 4,
        2 * rows * features * features,
        2 * features * features,
        grant=16,
    )(place, attended, received, out_weight, residual[0])

    groups = sections * cores
    grad_scale = 1.0 / float(groups * seqs * rows) ** 0.5
    side_x, side_y = 4, sections // 4
    lines = [
        [(x * side_y + y) for x in range(side_x)] for y in range(side_y)
    ]
    terms = lax.all_to_all(
        partial.reshape(side_x, side_y * width, half),
        "section",
        0,
        0,
        tiled=True,
        axis_index_groups=lines,
    )
    terms = call(
        first_sum_kernel,
        bf16(side_y * width, half),
        [VMEM],
        half * half,
        3 * half * half,
    )(terms)
    rows_of_chips = [[x * side_y + y for y in range(side_y)] for x in range(side_x)]
    terms = lax.all_to_all(
        terms.reshape(side_y, width, half),
        "section",
        0,
        0,
        tiled=True,
        axis_index_groups=rows_of_chips,
    )
    tall = 24
    terms = call(
        second_sum_kernel,
        bf16(units, tall, 128),
        [VMEM],
        side_y * width * half,
        3 * side_y * width * half,
    )(terms)
    same_side = [list(range(side, seqs, 2)) for side in range(2)]
    terms = lax.all_to_all(terms, "seq", 0, 0, tiled=True, axis_index_groups=same_side)
    spread = call(
        functools.partial(third_sum_kernel, grad_scale),
        bf16(seqs, tall, 128),
        [VMEM],
        units * tall * 128,
        2 * (units + seqs) * tall * 128,
    )(terms)
    spread = lax.all_to_all(spread, "seq", 0, 0, tiled=True)
    weight_grad = call(
        assembly_kernel,
        jax.ShapeDtypeStruct((width, features), jnp.float32),
        [VMEM],
        seqs * tall * 128,
        2 * seqs * tall * 128,
    )(spread)
    return (mixed_out[None], weight_grad)


def solution(mesh):
    in_specs = (
        P(("section", "dp"), "seq", None),
        P(("section", "dp"), "seq", None),
        P(("section", "dp"), "seq", None),
        P(("section", "dp"), "seq", None),
        P(("section", "dp"), None),
        P(),
        P(("section", "dp"), "seq", None),
    )
    out_specs = (P(("section", "dp"), "seq", None), P(("section", "dp"), None))
    return jax.shard_map(
        per_device, mesh=mesh, in_specs=in_specs, out_specs=out_specs, check_vma=False
    )
```

```python
import functools

import jax
import jax.numpy as jnp
from jax import lax
from jax.experimental import pallas as pl
from jax.experimental.pallas import tpu as pltpu
from jax.sharding import PartitionSpec as P


HEADS = 16
LOG2E = 1.4426950408889634
AXES = ("section", "seq", "dp")
ANY = pl.BlockSpec(memory_space=pl.ANY)
HBM = pl.BlockSpec(memory_space=pltpu.HBM)
VMEM = pl.BlockSpec(memory_space=pltpu.VMEM)
SMEM = pl.BlockSpec(memory_space=pltpu.SMEM)
NT = (((1,), (1,)), ((), ()))
TT = (((0,), (1,)), ((), ()))


def moved(value, target):
    sections, seqs, cores = (lax.axis_size(axis) for axis in AXES)
    pairs = []
    for section in range(sections):
        for seq in range(seqs):
            for core in range(cores):
                to_seq, to_core = target(seq, core)
                if 0 <= to_seq < seqs:
                    source = (section * seqs + seq) * cores + core
                    pairs.append((source, (section * seqs + to_seq) * cores + to_core))
    return lax.ppermute(value, AXES, pairs)


def to_pair(value):
    return moved(value, lambda seq, core: (seq ^ 1, core))


def to_core(value):
    return moved(value, lambda seq, core: (seq, 1 - core))


def to_next(value):
    return moved(value, lambda seq, core: (seq + 2, core))


def to_previous(value):
    return moved(value, lambda seq, core: (seq - 2, core))


def position(place):
    index = place[0]
    return index >> 2, (index >> 1) & 1, index & 1


def split_kernel(
    width, place, query, key, value, cotangent, kv_own, kv_other, q_own, q_other, exchanged
):
    _, y, _ = position(place)
    half = q_own.shape[1]
    own = pl.ds(pl.multiple_of(y * half, half), half)
    other = pl.ds(pl.multiple_of((1 - y) * half, half), half)
    for part, out in ((own, kv_own), (other, kv_other)):
        out[0] = key[:, part]
        chosen = value[:, part]
        for first in range(0, half, 128):
            out[1, :, first : first + 128] = jnp.transpose(chosen[:, first : first + 128])
    q_own[...] = query[:, own]
    q_other[...] = query[:, other]
    picked = half // 2
    shift = 20
    factor = -(-(1 << shift) // width)
    assert all((j * factor) >> shift == j // width for j in range(picked))
    row = lax.broadcasted_iota(jnp.int32, (picked, half), 0)
    column = lax.broadcasted_iota(jnp.int32, (picked, half), 1)
    base = row + lax.shift_right_logical(row * factor, shift) * width
    for to_core_index in range(2):
        chosen = (column == base + to_core_index * width).astype(jnp.float32)
        chosen = chosen.astype(jnp.bfloat16)
        for part in range(2):
            block = lax.dot_general(
                chosen,
                cotangent[:, part * half : (part + 1) * half],
                NT,
                preferred_element_type=jnp.float32,
            ).astype(jnp.bfloat16)
            for side in range(2):
                exchanged[
                    side * 2 + to_core_index, part * picked : (part + 1) * picked, :
                ] = block


def attention_kernel(
    head_dim, place, segments, q_own, q_pair, kv_own, kv_pair, kv_left, kv_left_pair,
    kv_right, kv_right_pair, attended, passed, queries, keys, values, bias, scores, probs, sems
):
    rows, half = q_own.shape
    total = segments.shape[1]
    heads = half // head_dim
    z, y, _ = position(place)
    blocks = (kv_own, kv_pair, kv_left, kv_left_pair, kv_right, kv_right_pair)
    moves = [(q_own, queries.at[pl.ds(0, rows)]), (q_pair, queries.at[pl.ds(rows, rows)])]
    for i, block in enumerate(blocks):
        here = pl.ds(i * rows, rows)
        moves.append((block.at[0], keys.at[here]))
        for first in range(0, half, 128):
            some = pl.ds(first, 128)
            moves.append((block.at[1, :, some], values.at[some, here]))
    copies = [
        pltpu.make_async_copy(source, target, sems.at[i])
        for i, (source, target) in enumerate(moves)
    ]
    for copy in copies:
        copy.start()
    ids = []
    for i in range(6):
        offset = ((z + (0, -1, 1)[i // 2]) * 2 + (y if i % 2 == 0 else 1 - y)) * rows
        start = pl.multiple_of(jnp.clip(offset, 0, total - rows), rows)
        row = segments[:, pl.ds(start, rows)]
        ids.append(jnp.where((offset >= 0) & (offset < total), row, -1))
    for i in range(6):
        key_ids = jnp.transpose(jnp.broadcast_to(ids[i], (rows, rows)))
        for j in range(2):
            bias[i * rows : (i + 1) * rows, j * rows : (j + 1) * rows] = jnp.where(
                key_ids == ids[j], jnp.float32(0.0), jnp.float32(-1e30)
            )
    for copy in copies:
        copy.wait()
    scale = head_dim ** (-0.5) * LOG2E
    ones = jnp.ones((16, 6 * rows), jnp.bfloat16)
    step = 64

    def multiply(head):
        first, last = head * head_dim, (head + 1) * head_dim
        low, high = first // 128 * 128, -(-last // 128) * 128
        lane = lax.broadcasted_iota(jnp.int32, (2 * rows, high - low), 1) + low
        inside = (lane >= first) & (lane < last)
        query = jnp.where(inside, queries[:, low:high], jnp.zeros((), jnp.bfloat16))
        found = lax.dot_general(
            keys[:, low:high], query, NT, preferred_element_type=jnp.float32
        )
        found = found + bias[...]
        scores[head % 2] = found
        return jnp.max(found, axis=0, keepdims=True)

    highest = multiply(0)
    for head in range(heads):
        following = multiply(head + 1) if head + 1 < heads else None
        for low in range(0, 6 * rows, step):
            some = slice(low, low + step)
            expo = jnp.exp2((scores[head % 2, some, :] - highest) * scale)
            probs[head % 2, some, :] = expo.astype(jnp.bfloat16)
        here = slice(head * head_dim, (head + 1) * head_dim)
        weighted = jnp.dot(
            jnp.concatenate([values[here, :], ones], axis=0),
            probs[head % 2],
            preferred_element_type=jnp.float32,
        )
        norm = 1.0 / weighted[head_dim : head_dim + 1, :]
        result = (weighted[:head_dim, :] * norm).astype(jnp.bfloat16)
        attended[here, :] = result
        passed[here, :] = result[:, rows:]
        highest = following


def gradient_kernel(place, att, att_core, exchanged, out):
    _, y, core = position(place)
    order = (2 * y + core, 2 * (1 - y) + core, 2 * y + 1 - core, 2 * (1 - y) + 1 - core)
    left = jnp.concatenate([exchanged[index] for index in order], axis=1)
    right = jnp.concatenate([att[...], att_core[...]], axis=1)
    out[...] = lax.dot_general(left, right, NT, preferred_element_type=jnp.float32).astype(
        jnp.bfloat16
    )


def first_sum_kernel(terms, out):
    total = sum(terms[i].astype(jnp.float32) for i in range(terms.shape[0]))
    tall = out.shape[1]
    for part in range(out.shape[0]):
        column, row = part // 2 * 128, part % 2 * tall
        if column < terms.shape[2]:
            tile = total[row : row + tall, column : column + 128]
            if tile.shape[0] < tall:
                tile = jnp.concatenate(
                    [tile, jnp.zeros((tall - tile.shape[0], 128), jnp.float32)], axis=0
                )
        else:
            tile = jnp.zeros((tall, 128), jnp.float32)
        out[part] = tile.astype(jnp.bfloat16)


def second_sum_kernel(scale, terms, out):
    total = sum(terms[i].astype(jnp.float32) for i in range(terms.shape[0])) * scale
    total = total.astype(jnp.bfloat16)
    for i in range(out.shape[0]):
        out[i] = total


def assembly_kernel(terms, out):
    width, features = out.shape
    tall = terms.shape[1]
    for side in range(2):
        for part in range(features // 128):
            row = part % 2 * tall
            rows = min(tall, width - row)
            column = side * (features // 2) + part // 2 * 128
            tile = terms[part * 2 + side].astype(jnp.float32)
            out[row : row + rows, column : column + 128] = tile[:rows, :]


def projection_kernel(place, attended, received, weight, residual, out):
    half, rows = received.shape
    _, y, _ = position(place)
    own = pl.ds(pl.multiple_of(y * half, half), half)
    other = pl.ds(pl.multiple_of((1 - y) * half, half), half)
    total = lax.dot_general(
        attended[:, :rows], weight[:, own], TT, preferred_element_type=jnp.float32
    )
    total += lax.dot_general(
        received[...], weight[:, other], TT, preferred_element_type=jnp.float32
    )
    out[...] = (residual[...].astype(jnp.float32) + total).astype(jnp.bfloat16)


def call(kernel, outs, in_specs, flops, moved_bytes, scratch=(), grant=16):
    return pl.pallas_call(
        kernel,
        out_shape=outs,
        in_specs=in_specs,
        out_specs=jax.tree.map(lambda _: VMEM, outs),
        scratch_shapes=scratch,
        cost_estimate=pl.CostEstimate(
            flops=flops, bytes_accessed=moved_bytes, transcendentals=0
        ),
        compiler_params=pltpu.CompilerParams(vmem_limit_bytes=grant << 20),
    )


def per_device(queries, key_input, value_input, residual, segments, out_weight, cotangent):
    rows, features = queries.shape[1], queries.shape[2]
    half = features // 2
    head_dim = features // HEADS
    sections, seqs, cores = (lax.axis_size(axis) for axis in AXES)
    units = seqs // 2
    width = features // (sections * cores)
    place = lax.axis_index(("seq", "dp")).astype(jnp.int32).reshape(1)

    def bf16(*shape):
        return jax.ShapeDtypeStruct(shape, jnp.bfloat16)

    kv_own, kv_other, q_own, q_other, exchanged = call(
        functools.partial(split_kernel, width),
        (
            bf16(2, rows, half),
            bf16(2, rows, half),
            bf16(rows, half),
            bf16(rows, half),
            bf16(4, half, rows),
        ),
        [SMEM, VMEM, VMEM, VMEM, VMEM],
        2 * half * features * rows,
        24 * rows * features,
        grant=62,
    )(place, queries[0], key_input[0], value_input[0], cotangent[0])
    kv_pair = to_pair(kv_other)
    kv_left = to_next(kv_own)
    kv_right = to_previous(kv_own)
    kv_left_pair = to_next(kv_pair)
    kv_right_pair = to_previous(kv_pair)
    q_pair = to_pair(q_other)
    quads = [list(range(first, first + 4)) for first in range(0, 2 * seqs, 4)]
    exchanged = lax.all_to_all(
        exchanged, ("seq", "dp"), 0, 0, tiled=True, axis_index_groups=quads
    )
    attended, passed = call(
        functools.partial(attention_kernel, head_dim),
        (bf16(half, 2 * rows), bf16(half, rows)),
        [SMEM, VMEM] + [ANY] * 8,
        4 * 2 * rows * 6 * rows * half,
        26 * rows * half,
        scratch=[
            pltpu.VMEM((2 * rows, half), jnp.bfloat16),
            pltpu.VMEM((6 * rows, half), jnp.bfloat16),
            pltpu.VMEM((half, 6 * rows), jnp.bfloat16),
            pltpu.VMEM((6 * rows, 2 * rows), jnp.float32),
            pltpu.VMEM((2, 6 * rows, 2 * rows), jnp.float32),
            pltpu.VMEM((2, 6 * rows, 2 * rows), jnp.bfloat16),
            pltpu.SemaphoreType.DMA((2 + 6 * (1 + half // 128),)),
        ],
        grant=16,
    )(
        place, segments, q_own, q_pair, kv_own, kv_pair, kv_left, kv_left_pair,
        kv_right, kv_right_pair,
    )
    attended_core = to_core(attended)
    received = to_pair(passed)
    partial = call(
        gradient_kernel,
        bf16(half, half),
        [SMEM, VMEM, VMEM, VMEM],
        2 * half * half * 4 * rows,
        2 * half * half,
        grant=62,
    )(place, attended, attended_core, exchanged)
    mixed_out = call(
        projection_kernel,
        bf16(rows, features),
        [SMEM] + [VMEM] * 4,
        2 * rows * features * features,
        2 * features * features,
        grant=16,
    )(place, attended, received, out_weight, residual[0])

    groups = sections * cores
    grad_scale = 1.0 / float(groups * seqs * rows) ** 0.5
    terms = lax.all_to_all(
        partial.reshape(sections, width, half), "section", 0, 0, tiled=True
    )
    tall = 24
    terms = call(
        first_sum_kernel,
        bf16(units, tall, 128),
        [VMEM],
        sections * width * half,
        3 * sections * width * half,
    )(terms)
    same_side = [list(range(side, seqs, 2)) for side in range(2)]
    terms = lax.all_to_all(terms, "seq", 0, 0, tiled=True, axis_index_groups=same_side)
    spread = call(
        functools.partial(second_sum_kernel, grad_scale),
        bf16(seqs, tall, 128),
        [VMEM],
        units * tall * 128,
        2 * (units + seqs) * tall * 128,
    )(terms)
    spread = lax.all_to_all(spread, "seq", 0, 0, tiled=True)
    weight_grad = call(
        assembly_kernel,
        jax.ShapeDtypeStruct((width, features), jnp.float32),
        [VMEM],
        seqs * tall * 128,
        2 * seqs * tall * 128,
    )(spread)
    return (mixed_out[None], weight_grad)


def solution(mesh):
    in_specs = (
        P(("section", "dp"), "seq", None),
        P(("section", "dp"), "seq", None),
        P(("section", "dp"), "seq", None),
        P(("section", "dp"), "seq", None),
        P(("section", "dp"), None),
        P(),
        P(("section", "dp"), "seq", None),
    )
    out_specs = (P(("section", "dp"), "seq", None), P(("section", "dp"), None))
    return jax.shard_map(
        per_device, mesh=mesh, in_specs=in_specs, out_specs=out_specs, check_vma=False
    )
```
